512 devices in a mesh: dp: 8 (over z_hi, x), row: 8 (over y, core), col: 8 (over z_lo).
Axes of the slice: x: 4, y: 4, z: 16 (z_hi: 2, z_lo: 8; z = z_hi * 8 + z_lo), core: 2. Of those that a mesh axis runs over, the one named last changes fastest.
Arguments:
- tokens: bfloat16 [65536, 8192], P(('dp', 'row', 'col')), parts along dimension 0, may hold values from -60 to 60
- norm_gain: float32 [8192], replicated, may hold values from 0.1 to 1.9
- w_key: bfloat16 [8192, 1024], P('row', 'col'), may hold values from -0.0625 to 0.0625
- w_value: bfloat16 [8192, 1024], P('row', 'col'), may hold values from -0.0625 to 0.0625
Outputs:
- key_rows: bfloat16 [65536, 1024], P(('dp', 'row', 'col')), parts along dimension 0
- value_rows: bfloat16 [65536, 1024], P(('dp', 'row', 'col')), parts along dimension 0
The draws below stay inside these ranges and needn't reach their ends.
There are 8 independent parts, one for each index of `dp`. The reference program is written for one: setup_inputs(seed, part) draws one part's arguments, and reference() takes and returns one part's arrays. A program takes and returns all parts, laid end to end along the dimension named above; an argument that names none is the same for every part. Nothing has to cross between parts.
All inputs are finite; a program needn't handle non-finite values.
Results may differ from the reference program's by a relative error of at most 0.014.
Values may be sent and summed in bfloat16 or wider, within the bound.
A program may use at most 64 MiB of HBM per device.

```python
import jax
import jax.numpy as jnp
from jax import lax

D = 8192
HEAD = 128
KVW = 1024
LEN = 8192
N_ROW = 8


def draw_tokens(key, part):
    key_base = jax.random.fold_in(key, 11)
    key_rows = jax.random.fold_in(key, 12)
    key_cols = jax.random.fold_in(key, 13)
    row_scales = jnp.exp(jax.random.uniform(key_rows, (LEN, 1), jnp.float32, -1.2, 1.2))
    col_scales = jnp.exp(jax.random.uniform(key_cols, (1, D), jnp.float32, -1.2, 1.2))
    entries = jnp.clip(jax.random.normal(key_base, (LEN, D), jnp.float32), -5.0, 5.0)
    return (entries * row_scales * col_scales).astype(jnp.bfloat16)


def levels(stream_key, dims, cuts, smallest, top_value):
    def one(dim, blocks):
        heights = jax.random.uniform(jax.random.fold_in(jax.random.fold_in(stream_key, 6), dim), (blocks,), jnp.float32, smallest / len(cuts), top_value / len(cuts))
        return jnp.repeat(jnp.exp(heights), dims[dim] // blocks).reshape((-1,) + (1,) * (len(dims) - dim - 1))

    level = one(*cuts[0])
    for cut in cuts[1:]:
        level = level * one(*cut)
    return level


def centred(stream_key, dims, scale, bound, split=(), kind=jnp.bfloat16):
    level = levels(stream_key, dims, split, -0.22, 0.18) if split else 1.0
    values = jax.random.normal(stream_key, dims, jnp.float32) * scale * level
    return jnp.minimum(jnp.maximum(values, -bound), bound).astype(kind)


def setup_inputs(seed: int = 0, part: int = 0) -> dict:
    key_list = jax.random.split(jax.random.key(seed), 5)
    part_splits = jax.random.split(jax.random.fold_in(key_list[4], part), 5)
    return {
        "tokens": draw_tokens(jax.random.fold_in(jax.random.fold_in(key_list[4], part), 71), part),
        "norm_gain": jnp.clip(1.0 + 0.18 * jax.random.normal(key_list[1], (D,), jnp.float32), 0.1, 1.9),
        "w_key": centred(key_list[2], (D, KVW), D ** -0.5, 0.0625, ((0, 8), (1, 8))),
        "w_value": centred(key_list[3], (D, KVW), D ** -0.5, 0.0625, ((0, 8), (1, 8))),
    }


rope_base = 500000.0

def rotate(projected, positions):
    row_count = projected.shape[0]
    head_count = projected.shape[1] // HEAD
    half_head = HEAD // 2
    frequency = rope_base ** (-2.0 * jnp.arange(half_head, dtype=jnp.float32) / HEAD)
    angles = positions.astype(jnp.float32)[:, None] * frequency[None, :]
    cosine = jnp.cos(angles)[:, None, :]
    sine = jnp.sin(angles)[:, None, :]
    split_heads = projected.reshape(row_count, head_count, HEAD)
    first = split_heads[:, :, :half_head]
    second = split_heads[:, :, half_head:]
    turned = jnp.concatenate([first * cosine - second * sine, second * cosine + first * sine], axis=2)
    return turned.reshape(row_count, head_count * HEAD)

def reference(tokens, norm_gain, w_key, w_value):
    widened = tokens.astype(jnp.float32)
    inverse_rms = lax.rsqrt(lax.optimization_barrier(jnp.mean(widened * widened, axis=1, keepdims=True)) + 1e-05)
    normed = (widened * inverse_rms * norm_gain.astype(jnp.float32)[None, :]).astype(jnp.bfloat16)
    weights = jnp.concatenate([w_key, w_value], axis=1)
    block = D // N_ROW

    def add_block(total, index):
        start = (index * block).astype(jnp.int32)
        rows = lax.dynamic_slice_in_dim(normed, start, block, 1)
        piece = lax.dynamic_slice_in_dim(weights, start, block, 0)
        partial_sum = jnp.dot(rows, piece, preferred_element_type=jnp.float32).astype(jnp.bfloat16)
        partial_sum = lax.optimization_barrier(partial_sum)
        return (total + partial_sum.astype(jnp.float32), None)
    start_total = jnp.zeros((LEN, 2 * KVW), jnp.float32)
    summed, unused = lax.scan(add_block, start_total, jnp.arange(N_ROW, dtype=jnp.int32))
    positions = jnp.arange(LEN, dtype=jnp.int32)
    key_rows = rotate(summed[:, :KVW], positions).astype(jnp.bfloat16)
    value_rows = summed[:, KVW:].astype(jnp.bfloat16)
    return (key_rows, value_rows)
```

```python
import functools

import jax
import jax.numpy as jnp
from jax import lax
from jax.experimental import pallas as pl
from jax.experimental.pallas import tpu as pltpu
from jax.sharding import PartitionSpec as P

HEAD = 128
EPS = 1e-05
MESH = pl.DeviceIdType.MESH

rope_base = 500000.0

UNITS = (0, 1, 7, 2, 6, 3, 5, 4)


def rotation_tables(positions):
    half_head = HEAD // 2
    frequency = rope_base ** (-2.0 * jnp.arange(half_head, dtype=jnp.float32) / HEAD)
    angles = positions.astype(jnp.float32)[:, None] * frequency[None, :]
    cosine = jnp.cos(angles)
    sine = jnp.sin(angles)
    return (
        jnp.concatenate([cosine, cosine], axis=1),
        jnp.concatenate([-sine, sine], axis=1),
    )


def kernel(
    tokens, gain, w_key, w_value, cosine, sine, key_out, value_out,
    tok, tile, weights, hop, kept, pair_out, pair_in, far_out, far_in, near_out, near_in, scale,
    local_sem, z_send, z_recv, hop_send, hop_recv, tile_send, tile_recv,
    pair_send, pair_recv, far_send, far_recv, near_send, near_recv,
):
    rows = tokens.shape[0]
    depth, width = w_key.shape
    half = rows // 2
    dp, row, col = lax.axis_index("dp"), lax.axis_index("row"), lax.axis_index("col")
    y, core = row // 2, row % 2
    other = 1 - core

    def at(step, which):
        return (dp, ((y + step + 4) % 4) * 2 + which, col)

    wrap_up, wrap_down = col // 7, (7 - col) // 7
    z_next = ((dp + 4 * wrap_up) % 8, row, (col + 1) % 8)
    z_prev = ((dp + 4 * wrap_down) % 8, row, (col + 7) % 8)

    partners = [at(1, core), at(3, core), at(1, other), at(3, other), at(0, other), z_next, z_prev]
    barrier = pltpu.get_barrier_semaphore()
    for partner in partners:
        pl.semaphore_signal(barrier, inc=1, device_id=partner, device_id_type=MESH)
    pl.semaphore_wait(barrier, len(partners))

    sent = []

    def remote(src, dst, send, recv, device):
        return pltpu.make_async_remote_copy(
            src_ref=src, dst_ref=dst, send_sem=send, recv_sem=recv, device_id=device, device_id_type=MESH
        )

    def go(copy):
        copy.start()
        sent.append(copy)
        return copy

    def features(step, which):
        index = ((y + step) % 4) * 2 + which
        return tokens.at[:, pl.ds(pl.multiple_of(index * depth, depth), depth)]

    def tile_rows(kind, step):
        return tile.at[pl.ds((kind * 4 + step) * rows, rows), :]

    def piece(way, j):
        distance = j // 2 + 1
        kind = (j + way) % 2
        columns = pl.ds(kind * width, width)
        to = distance if way == 0 else 8 - distance
        back = (distance - 1) if way == 0 else (9 - distance) % 8
        src = (w_key, w_value)[kind] if distance == 1 else weights.at[back, :, columns]
        return remote(
            src, weights.at[to, :, columns], z_send.at[way, j], z_recv.at[way, j], (z_next, z_prev)[way]
        )

    pieces = [[piece(way, j) for j in range(7)] for way in range(2)]
    for j in range(2):
        for way in range(2):
            go(pieces[way][j])
    hops = [
        go(remote(features(2, core), hop.at[0], hop_send.at[0], hop_recv.at[0], at(1, core))),
        go(remote(features(2, other), hop.at[1], hop_send.at[1], hop_recv.at[1], at(3, core))),
    ]
    blocks = {}
    for kind, step in ((0, 1), (0, 3), (1, 1), (1, 3), (1, 0)):
        which = other if kind else core
        slot = (4 - step) % 4
        blocks[kind, slot] = go(
            remote(features(step, which), tile_rows(kind, slot), tile_send.at[kind, slot], tile_recv.at[kind, slot], at(step, which))
        )
    own_tile = pltpu.make_async_copy(features(0, core), tile_rows(0, 0), local_sem.at[0])
    own_key = pltpu.make_async_copy(w_key, weights.at[0, :, pl.ds(0, width)], local_sem.at[1])
    own_value = pltpu.make_async_copy(w_value, weights.at[0, :, pl.ds(width, width)], local_sem.at[2])
    own_tokens = pltpu.make_async_copy(tokens, tok, local_sem.at[3])
    for copy in (own_tokens, own_tile, own_key, own_value):
        copy.start()

    own_tokens.wait()

    def squares(i, total):
        part = tok[:, pl.ds(pl.multiple_of(i * 128, 128), 128)].astype(jnp.float32)
        return total + part * part

    total = lax.fori_loop(0, tokens.shape[1] // 128, squares, jnp.zeros((rows, 128), jnp.float32))
    mean = jnp.sum(total, axis=1, keepdims=True) / tokens.shape[1]
    scale[...] = jnp.broadcast_to(lax.rsqrt(mean + EPS), scale.shape)

    own_gain = gain[:, pl.ds(pl.multiple_of(row * depth, depth), depth)]

    def weigh(kind, step):
        ref = tile_rows(kind, step)
        ref[...] = (ref[...].astype(jnp.float32) * own_gain).astype(jnp.bfloat16)

    def arrive(j):
        for way in range(2):
            pieces[way][j].wait_recv()
            if j + 2 < 7:
                go(pieces[way][j + 2])

    arrive(0)
    hops[0].wait_recv()
    blocks[0, 2] = go(remote(hop.at[0], tile_rows(0, 2), tile_send.at[0, 2], tile_recv.at[0, 2], at(1, core)))
    hops[1].wait_recv()
    blocks[1, 2] = go(remote(hop.at[1], tile_rows(1, 2), tile_send.at[1, 2], tile_recv.at[1, 2], at(3, other)))
    own_tile.wait()
    weigh(0, 0)
    blocks[1, 0].wait_recv()
    weigh(1, 0)
    arrive(1)
    for slot in (1, 3):
        blocks[0, slot].wait_recv()
        weigh(0, slot)
    arrive(2)
    for slot in (1, 3):
        blocks[1, slot].wait_recv()
        weigh(1, slot)
    arrive(3)
    for kind in (1, 0):
        blocks[kind, 2].wait_recv()
        weigh(kind, 2)
    own_key.wait()
    own_value.wait()

    pairs, fars, nears = {}, {}, {}

    def multiply(u):
        w = weights[UNITS[u]]
        pair_out[u] = jnp.dot(
            tile[pl.ds(4 * rows, 4 * rows), :], w, preferred_element_type=jnp.float32
        ).astype(jnp.bfloat16)
        pairs[u] = go(remote(pair_out.at[u], pair_in.at[u], pair_send.at[u], pair_recv.at[u], at(0, other)))
        kept[u] = jnp.dot(tile[pl.ds(0, 4 * rows), :], w, preferred_element_type=jnp.float32)

    def chip_sum(u, step, low, size):
        at_rows = pl.ds(step * rows + low, size)
        return kept[u, at_rows, :] + pair_in[u, at_rows, :].astype(jnp.float32)

    def relay(u):
        pairs[u].wait_recv()
        for way in range(2):
            far_out[u, way] = chip_sum(u, 2, way * half, half).astype(jnp.bfloat16)
            fars[u, way] = go(
                remote(far_out.at[u, way], far_in.at[u, way], far_send.at[u, way], far_recv.at[u, way], at((1, 3)[way], core))
            )

    def neighbour(u):
        for way in range(2):
            step = (1, 3)[way]
            fars[u, way].wait_recv()
            mine, through = pl.ds((1 - way) * half, half), pl.ds(way * half, half)
            near_out[u, way, mine, :] = chip_sum(u, step, (1 - way) * half, half).astype(jnp.bfloat16)
            near_out[u, way, through, :] = (
                chip_sum(u, step, way * half, half) + far_in[u, way].astype(jnp.float32)
            ).astype(jnp.bfloat16)
            nears[u, way] = go(
                remote(near_out.at[u, way], near_in.at[u, way], near_send.at[u, way], near_recv.at[u, way], at(step, core))
            )

    def finish(u):
        result = chip_sum(u, 0, 0, rows)
        for way in range(2):
            nears[u, way].wait_recv()
            result = result + near_in[u, way].astype(jnp.float32)
        key, value = result[:, :width] * scale[...], result[:, width:] * scale[...]
        turned = key * cosine[...] + pltpu.roll(key, HEAD // 2, 1) * sine[...]
        columns = pl.ds(pl.multiple_of(((col + 8 - UNITS[u]) % 8) * width, width), width)
        key_out[:, columns] = turned.astype(jnp.bfloat16)
        value_out[:, columns] = value.astype(jnp.bfloat16)

    count = len(UNITS)
    for step in range(count + 3):
        if step == 5:
            arrive(5)
        if step == 7:
            arrive(6)
        if step < count:
            multiply(step)
        if step == 2:
            arrive(4)
        if 0 <= step - 1 < count:
            relay(step - 1)
        if 0 <= step - 2 < count:
            neighbour(step - 2)
        if 0 <= step - 3 < count:
            finish(step - 3)
    for copy in sent:
        copy.wait_send()


def body(tokens, norm_gain, w_key, w_value):
    rows, model = tokens.shape
    depth, width = w_key.shape
    pair = 2 * width
    first = (lax.axis_index("row") * lax.axis_size("col") + lax.axis_index("col")) * rows
    cosine, sine = rotation_tables(first + jnp.arange(rows, dtype=jnp.int32))
    units = len(UNITS)
    bf16, f32 = jnp.bfloat16, jnp.float32
    dma = pltpu.SemaphoreType.DMA
    anywhere = pl.BlockSpec(memory_space=pl.ANY)
    vmem = pl.BlockSpec(memory_space=pltpu.VMEM)
    out = jax.ShapeDtypeStruct((rows, units * width), bf16)
    return pl.pallas_call(
        kernel,
        name="key_value",
        out_shape=(out, out),
        in_specs=[anywhere, vmem, anywhere, anywhere, vmem, vmem],
        out_specs=(vmem, vmem),
        scratch_shapes=[
            pltpu.VMEM((rows, model), bf16),
            pltpu.VMEM((8 * rows, depth), bf16),
            pltpu.VMEM((units, depth, pair), bf16),
            pltpu.VMEM((2, rows, depth), bf16),
            pltpu.VMEM((units, 4 * rows, pair), f32),
            pltpu.VMEM((units, 4 * rows, pair), bf16),
            pltpu.VMEM((units, 4 * rows, pair), bf16),
            pltpu.VMEM((units, 2, rows // 2, pair), bf16),
            pltpu.VMEM((units, 2, rows // 2, pair), bf16),
            pltpu.VMEM((units, 2, rows, pair), bf16),
            pltpu.VMEM((units, 2, rows, pair), bf16),
            pltpu.VMEM((rows, width), f32),
            dma((4,)),
            dma((2, 7)), dma((2, 7)),
            dma((2,)), dma((2,)),
            dma((2, 4)), dma((2, 4)),
            dma((units,)), dma((units,)),
            dma((units, 2)), dma((units, 2)),
            dma((units, 2)), dma((units, 2)),
        ],
        compiler_params=pltpu.CompilerParams(collective_id=0, has_side_effects=True),
    )(tokens, norm_gain.reshape(1, model), w_key, w_value, cosine, sine)


def solution(mesh):
    placed = (P(("dp", "row", "col"), None), P(), P("row", "col"), P("row", "col"))
    return jax.shard_map(
        body,
        mesh=mesh,
        in_specs=placed,
        out_specs=(P(("dp", "row", "col"), None), P(("dp", "row", "col"), None)),
        check_vma=False,
    )
```

```python
import jax
import jax.numpy as jnp
import numpy as np
from jax import lax
from jax.experimental import pallas as pl
from jax.experimental.pallas import tpu as pltpu
from jax.sharding import PartitionSpec as P

HEAD = 128
EPS = 1e-05
MESH = pl.DeviceIdType.MESH

rope_base = 500000.0

UNITS = (0, 1, 7, 2, 6, 3, 5, 4)


def rotation_tables(first, frequency, shape):
    lane = lax.broadcasted_iota(jnp.int32, shape, 1)
    position = first + lax.broadcasted_iota(jnp.int32, shape, 0)
    angles = position.astype(jnp.float32) * frequency
    sine = jnp.sin(angles)
    return jnp.cos(angles), jnp.where(lane < HEAD // 2, -sine, sine)


def kernel(
    tokens, gain, w_key, w_value, frequency, key_out, value_out,
    tok, tile, weights, hop, kept, pair_out, pair_in, far_out, far_in, near_out, near_in, scale, cosine, sine,
    local_sem, z_send, z_recv, x_send, x_recv, hop_send, hop_recv, tile_send, tile_recv,
    pair_send, pair_recv, far_send, far_recv, near_send, near_recv,
):
    rows = tokens.shape[0]
    depth, width = w_key.shape
    half = rows // 2
    dp, row, col = lax.axis_index("dp"), lax.axis_index("row"), lax.axis_index("col")
    y, core = row // 2, row % 2
    other = 1 - core

    def at(step, which):
        return (dp, ((y + step + 4) % 4) * 2 + which, col)

    wrap_up, wrap_down = col // 7, (7 - col) // 7
    z_next = ((dp + 4 * wrap_up) % 8, row, (col + 1) % 8)
    z_prev = ((dp + 4 * wrap_down) % 8, row, (col + 7) % 8)

    x, kind_here = dp % 4, dp % 2
    x_next = (dp - x + (x + 1) % 4, row, col)
    x_prev = (dp - x + (x + 3) % 4, row, col)

    partners = [at(1, core), at(3, core), at(1, other), at(3, other), at(0, other), z_next, z_prev, x_next, x_prev]
    def features(step, which):
        index = ((y + step) % 4) * 2 + which
        return tokens.at[:, pl.ds(pl.multiple_of(index * depth, depth), depth)]

    def tile_rows(kind, step):
        return tile.at[pl.ds((kind * 4 + step) * rows, rows), :]

    own_key = pltpu.make_async_copy(w_key, weights.at[0, :, pl.ds(0, width)], local_sem.at[1])
    own_value = pltpu.make_async_copy(w_value, weights.at[0, :, pl.ds(width, width)], local_sem.at[2])
    own_tile = pltpu.make_async_copy(features(0, core), tile_rows(0, 0), local_sem.at[0])
    own_tokens = pltpu.make_async_copy(tokens, tok, local_sem.at[3])
    for copy in (own_key, own_value, own_tile, own_tokens):
        copy.start()

    barrier = pltpu.get_barrier_semaphore()
    for partner in partners:
        pl.semaphore_signal(barrier, inc=1, device_id=partner, device_id_type=MESH)
    pl.semaphore_wait(barrier, len(partners))

    sent = []

    def remote(src, dst, send, recv, device):
        return pltpu.make_async_remote_copy(
            src_ref=src, dst_ref=dst, send_sem=send, recv_sem=recv, device_id=device, device_id_type=MESH
        )

    def go(copy):
        copy.start()
        sent.append(copy)
        return copy

    def columns_of(kind):
        return pl.ds(pl.multiple_of(kind * width, width), width)

    def part(slot, j, way, kind):
        return weights.at[slot, pl.ds(((j + way) % 2) * (depth // 2), depth // 2), columns_of(kind)]

    def slot_of(way, distance):
        return distance if way == 0 else (8 - distance) % 8

    def piece(way, j):
        distance = j // 2 + 1
        return remote(
            part(slot_of(way, distance - 1), j, way, kind_here), part(slot_of(way, distance), j, way, kind_here),
            z_send.at[way, j], z_recv.at[way, j], (z_next, z_prev)[way],
        )

    def across(way, j, kind):
        block = part(slot_of(way, j // 2 + 1), j, way, kind)
        return remote(block, block, x_send.at[way, j], x_recv.at[way, j], (x_next, x_prev)[(j + way) % 2])

    own_key.wait()
    own_value.wait()
    pieces = [[piece(way, j) for j in range(7)] for way in range(2)]
    for j in range(2):
        for way in range(2):
            go(pieces[way][j])
    hops = [
        go(remote(features(2, core), hop.at[0], hop_send.at[0], hop_recv.at[0], at(1, core))),
        go(remote(features(2, other), hop.at[1], hop_send.at[1], hop_recv.at[1], at(3, core))),
    ]
    blocks = {}
    for kind, step in ((0, 1), (0, 3), (1, 1), (1, 3), (1, 0)):
        which = other if kind else core
        slot = (4 - step) % 4
        blocks[kind, slot] = go(
            remote(features(step, which), tile_rows(kind, slot), tile_send.at[kind, slot], tile_recv.at[kind, slot], at(step, which))
        )

    own_tokens.wait()

    def squares(i, total):
        part = tok[:, pl.ds(pl.multiple_of(i * 128, 128), 128)].astype(jnp.float32)
        return total + part * part

    total = lax.fori_loop(0, tokens.shape[1] // 128, squares, jnp.zeros((rows, 128), jnp.float32))
    mean = jnp.sum(total, axis=1, keepdims=True) / tokens.shape[1]
    scale[...] = jnp.broadcast_to(lax.rsqrt(mean + EPS), scale.shape)

    first = (row * 8 + col) * rows
    cosine[...], sine[...] = rotation_tables(first, frequency[...], cosine.shape)

    own_gain = gain[:, pl.ds(pl.multiple_of(row * depth, depth), depth)]

    def weigh(kind, step):
        ref = tile_rows(kind, step)
        ref[...] = (ref[...].astype(jnp.float32) * own_gain).astype(jnp.bfloat16)

    def arrive(j):
        for way in range(2):
            pieces[way][j].wait_recv()
            if j + 2 < 7:
                go(pieces[way][j + 2])
            go(across(way, j, kind_here))

    def cross(j):
        for way in range(2):
            across(way, j, 1 - kind_here).wait_recv()

    arrive(0)
    hops[0].wait_recv()
    blocks[0, 2] = go(remote(hop.at[0], tile_rows(0, 2), tile_send.at[0, 2], tile_recv.at[0, 2], at(1, core)))
    hops[1].wait_recv()
    blocks[1, 2] = go(remote(hop.at[1], tile_rows(1, 2), tile_send.at[1, 2], tile_recv.at[1, 2], at(3, other)))
    arrive(1)
    own_tile.wait()
    weigh(0, 0)
    blocks[1, 0].wait_recv()
    weigh(1, 0)
    arrive(2)
    for slot in (1, 3):
        blocks[0, slot].wait_recv()
        weigh(0, slot)
    arrive(3)
    arrive(4)
    for slot in (1, 3):
        blocks[1, slot].wait_recv()
        weigh(1, slot)
    for kind in (1, 0):
        blocks[kind, 2].wait_recv()
        weigh(kind, 2)
    arrive(5)

    pairs, fars, nears = {}, {}, {}

    def multiply(u):
        w = weights[UNITS[u]]
        pair_out[u] = jnp.dot(
            tile[pl.ds(4 * rows, 4 * rows), :], w, preferred_element_type=jnp.float32
        ).astype(jnp.bfloat16)
        pairs[u] = go(remote(pair_out.at[u], pair_in.at[u], pair_send.at[u], pair_recv.at[u], at(0, other)))
        kept[u] = jnp.dot(tile[pl.ds(0, 4 * rows), :], w, preferred_element_type=jnp.float32)

    def chip_sum(u, step, low, size):
        at_rows = pl.ds(step * rows + low, size)
        return kept[u, at_rows, :] + pair_in[u, at_rows, :].astype(jnp.float32)

    def relay(u):
        pairs[u].wait_recv()
        for way in range(2):
            far_out[u, way] = chip_sum(u, 2, way * half, half).astype(jnp.bfloat16)
            fars[u, way] = go(
                remote(far_out.at[u, way], far_in.at[u, way], far_send.at[u, way], far_recv.at[u, way], at((1, 3)[way], core))
            )

    def neighbour(u):
        for way in range(2):
            step = (1, 3)[way]
            fars[u, way].wait_recv()
            mine, through = pl.ds((1 - way) * half, half), pl.ds(way * half, half)
            near_out[u, way, mine, :] = chip_sum(u, step, (1 - way) * half, half).astype(jnp.bfloat16)
            near_out[u, way, through, :] = (
                chip_sum(u, step, way * half, half) + far_in[u, way].astype(jnp.float32)
            ).astype(jnp.bfloat16)
            nears[u, way] = go(
                remote(near_out.at[u, way], near_in.at[u, way], near_send.at[u, way], near_recv.at[u, way], at(step, core))
            )

    def finish(u):
        result = chip_sum(u, 0, 0, rows)
        for way in range(2):
            nears[u, way].wait_recv()
            result = result + near_in[u, way].astype(jnp.float32)
        key, value = result[:, :width] * scale[...], result[:, width:] * scale[...]
        turned = key * cosine[...] + pltpu.roll(key, HEAD // 2, 1) * sine[...]
        columns = pl.ds(pl.multiple_of(((col + 8 - UNITS[u]) % 8) * width, width), width)
        key_out[:, columns] = turned.astype(jnp.bfloat16)
        value_out[:, columns] = value.astype(jnp.bfloat16)

    count = len(UNITS)
    for step in range(count + 3):
        if step == 1:
            arrive(6)
        for j in {1: (0, 1), 3: (2, 3), 5: (4, 5), 7: (6,)}.get(step, ()):
            cross(j)
        if step < count:
            multiply(step)
        if 0 <= step - 1 < count:
            relay(step - 1)
        if 0 <= step - 2 < count:
            neighbour(step - 2)
        if 0 <= step - 3 < count:
            finish(step - 3)
    for copy in sent:
        copy.wait_send()


def body(tokens, norm_gain, w_key, w_value):
    rows, model = tokens.shape
    depth, width = w_key.shape
    pair = 2 * width
    half_lane = np.arange(HEAD) % (HEAD // 2)
    frequency = jnp.asarray(rope_base ** (-2.0 * half_lane / HEAD), jnp.float32).reshape(1, HEAD)
    units = len(UNITS)
    bf16, f32 = jnp.bfloat16, jnp.float32
    dma = pltpu.SemaphoreType.DMA
    anywhere = pl.BlockSpec(memory_space=pl.ANY)
    vmem = pl.BlockSpec(memory_space=pltpu.VMEM)
    out = jax.ShapeDtypeStruct((rows, units * width), bf16)
    return pl.pallas_call(
        kernel,
        name="key_value",
        out_shape=(out, out),
        in_specs=[anywhere, vmem, anywhere, anywhere, vmem],
        out_specs=(vmem, vmem),
        scratch_shapes=[
            pltpu.VMEM((rows, model), bf16),
            pltpu.VMEM((8 * rows, depth), bf16),
            pltpu.VMEM((units, depth, pair), bf16),
            pltpu.VMEM((2, rows, depth), bf16),
            pltpu.VMEM((units, 4 * rows, pair), f32),
            pltpu.VMEM((units, 4 * rows, pair), bf16),
            pltpu.VMEM((units, 4 * rows, pair), bf16),
            pltpu.VMEM((units, 2, rows // 2, pair), bf16),
            pltpu.VMEM((units, 2, rows // 2, pair), bf16),
            pltpu.VMEM((units, 2, rows, pair), bf16),
            pltpu.VMEM((units, 2, rows, pair), bf16),
            pltpu.VMEM((rows, width), f32),
            pltpu.VMEM((rows, width), f32),
            pltpu.VMEM((rows, width), f32),
            dma((4,)),
            dma((2, 7)), dma((2, 7)),
            dma((2, 7)), dma((2, 7)),
            dma((2,)), dma((2,)),
            dma((2, 4)), dma((2, 4)),
            dma((units,)), dma((units,)),
            dma((units, 2)), dma((units, 2)),
            dma((units, 2)), dma((units, 2)),
        ],
        compiler_params=pltpu.CompilerParams(collective_id=0, has_side_effects=True),
    )(tokens, norm_gain.reshape(1, model), w_key, w_value, frequency)


def solution(mesh):
    placed = (P(("dp", "row", "col"), None), P(), P("row", "col"), P("row", "col"))
    return jax.shard_map(
        body,
        mesh=mesh,
        in_specs=placed,
        out_specs=(P(("dp", "row", "col"), None), P(("dp", "row", "col"), None)),
        check_vma=False,
    )
```

```python
import jax
import jax.numpy as jnp
import numpy as np
from jax import lax
from jax.experimental import pallas as pl
from jax.experimental.pallas import tpu as pltpu
from jax.sharding import PartitionSpec as P

HEAD = 128
EPS = 1e-05
MESH = pl.DeviceIdType.MESH

rope_base = 500000.0

UNITS = (0, 1, 7, 2, 6, 3, 5, 4)


def rotation_tables(first, frequency, shape):
    lane = lax.broadcasted_iota(jnp.int32, shape, 1)
    position = first + lax.broadcasted_iota(jnp.int32, shape, 0)
    angles = position.astype(jnp.float32) * frequency
    sine = jnp.sin(angles)
    return jnp.cos(angles), jnp.where(lane < HEAD // 2, -sine, sine)


def kernel(
    tokens, gain, w_key, w_value, frequency, key_out, value_out,
    tok, tile, weights, hop, kept, pair_out, pair_in, far_out, far_in, near_out, near_in, scale, cosine, sine, own_gain, own_frequency,
    local_sem, z_send, z_recv, x_send, x_recv, hop_send, hop_recv, tile_send, tile_recv,
    pair_send, pair_recv, far_send, far_recv, near_send, near_recv,
):
    rows = tokens.shape[0]
    depth, width = w_key.shape
    half = rows // 2
    dp, row, col = lax.axis_index("dp"), lax.axis_index("row"), lax.axis_index("col")
    y, core = row // 2, row % 2
    other = 1 - core

    def at(step, which):
        return (dp, ((y + step + 4) % 4) * 2 + which, col)

    wrap_up, wrap_down = col // 7, (7 - col) // 7
    z_next = ((dp + 4 * wrap_up) % 8, row, (col + 1) % 8)
    z_prev = ((dp + 4 * wrap_down) % 8, row, (col + 7) % 8)

    x, kind_here = dp % 4, dp % 2
    x_next = (dp - x + (x + 1) % 4, row, col)
    x_prev = (dp - x + (x + 3) % 4, row, col)

    partners = [at(1, core), at(3, core), at(1, other), at(3, other), at(0, other), z_next, z_prev, x_next, x_prev]
    def features(step, which):
        index = ((y + step) % 4) * 2 + which
        return tokens.at[:, pl.ds(pl.multiple_of(index * depth, depth), depth)]

    def tile_rows(kind, step):
        return tile.at[pl.ds((kind * 4 + step) * rows, rows), :]

    own_key = pltpu.make_async_copy(w_key, weights.at[0, :, pl.ds(0, width)], local_sem.at[1])
    own_value = pltpu.make_async_copy(w_value, weights.at[0, :, pl.ds(width, width)], local_sem.at[2])
    own_tile = pltpu.make_async_copy(features(0, core), tile_rows(0, 0), local_sem.at[0])
    own_tokens = pltpu.make_async_copy(tokens, tok, local_sem.at[3])
    gains = pltpu.make_async_copy(
        gain.at[:, pl.ds(pl.multiple_of(row * depth, depth), depth)], own_gain, local_sem.at[4]
    )
    frequencies = pltpu.make_async_copy(frequency, own_frequency, local_sem.at[5])
    for copy in (own_key, own_value, own_tile, own_tokens, gains, frequencies):
        copy.start()

    barrier = pltpu.get_barrier_semaphore()
    for partner in partners:
        pl.semaphore_signal(barrier, inc=1, device_id=partner, device_id_type=MESH)
    pl.semaphore_wait(barrier, len(partners))

    sent = []

    def remote(src, dst, send, recv, device):
        return pltpu.make_async_remote_copy(
            src_ref=src, dst_ref=dst, send_sem=send, recv_sem=recv, device_id=device, device_id_type=MESH
        )

    def go(copy):
        copy.start()
        sent.append(copy)
        return copy

    def columns_of(kind):
        return pl.ds(pl.multiple_of(kind * width, width), width)

    def part(slot, j, way, kind):
        return weights.at[slot, pl.ds(((j + way) % 2) * (depth // 2), depth // 2), columns_of(kind)]

    def slot_of(way, distance):
        return distance if way == 0 else (8 - distance) % 8

    def piece(way, j):
        distance = j // 2 + 1
        return remote(
            part(slot_of(way, distance - 1), j, way, kind_here), part(slot_of(way, distance), j, way, kind_here),
            z_send.at[way, j], z_recv.at[way, j], (z_next, z_prev)[way],
        )

    def across(way, j, kind):
        block = part(slot_of(way, j // 2 + 1), j, way, kind)
        return remote(block, block, x_send.at[way, j], x_recv.at[way, j], (x_next, x_prev)[(j + way) % 2])

    own_key.wait()
    own_value.wait()
    pieces = [[piece(way, j) for j in range(7)] for way in range(2)]
    for j in range(2):
        for way in range(2):
            go(pieces[way][j])
    hops = [
        go(remote(features(2, core), hop.at[0], hop_send.at[0], hop_recv.at[0], at(1, core))),
        go(remote(features(2, other), hop.at[1], hop_send.at[1], hop_recv.at[1], at(3, core))),
    ]
    blocks = {}
    for kind, step in ((0, 1), (0, 3), (1, 1), (1, 3), (1, 0)):
        which = other if kind else core
        slot = (4 - step) % 4
        blocks[kind, slot] = go(
            remote(features(step, which), tile_rows(kind, slot), tile_send.at[kind, slot], tile_recv.at[kind, slot], at(step, which))
        )

    own_tokens.wait()

    def squares(i, total):
        part = tok[:, pl.ds(pl.multiple_of(i * 128, 128), 128)].astype(jnp.float32)
        return total + part * part

    total = lax.fori_loop(0, tokens.shape[1] // 128, squares, jnp.zeros((rows, 128), jnp.float32))
    mean = jnp.sum(total, axis=1, keepdims=True) / tokens.shape[1]
    scale[...] = jnp.broadcast_to(lax.rsqrt(mean + EPS), scale.shape)

    frequencies.wait()
    gains.wait()
    first = (row * 8 + col) * rows
    cosine[...], sine[...] = rotation_tables(first, own_frequency[...], cosine.shape)

    def weigh(kind, step):
        ref = tile_rows(kind, step)
        ref[...] = (ref[...].astype(jnp.float32) * own_gain[...]).astype(jnp.bfloat16)

    def arrive(j):
        for way in range(2):
            pieces[way][j].wait_recv()
            if j + 2 < 7:
                go(pieces[way][j + 2])
            go(across(way, j, kind_here))

    def cross(j):
        for way in range(2):
            across(way, j, 1 - kind_here).wait_recv()

    arrive(0)
    hops[0].wait_recv()
    blocks[0, 2] = go(remote(hop.at[0], tile_rows(0, 2), tile_send.at[0, 2], tile_recv.at[0, 2], at(1, core)))
    hops[1].wait_recv()
    blocks[1, 2] = go(remote(hop.at[1], tile_rows(1, 2), tile_send.at[1, 2], tile_recv.at[1, 2], at(3, other)))
    arrive(1)
    own_tile.wait()
    weigh(0, 0)
    blocks[1, 0].wait_recv()
    weigh(1, 0)
    arrive(2)
    for slot in (1, 3):
        blocks[0, slot].wait_recv()
        weigh(0, slot)
    arrive(3)
    arrive(4)
    for slot in (1, 3):
        blocks[1, slot].wait_recv()
        weigh(1, slot)
    for kind in (1, 0):
        blocks[kind, 2].wait_recv()
        weigh(kind, 2)
    arrive(5)

    pairs, fars, nears = {}, {}, {}

    def multiply(u):
        w = weights[UNITS[u]]
        pair_out[u] = jnp.dot(
            tile[pl.ds(4 * rows, 4 * rows), :], w, preferred_element_type=jnp.float32
        ).astype(jnp.bfloat16)
        pairs[u] = go(remote(pair_out.at[u], pair_in.at[u], pair_send.at[u], pair_recv.at[u], at(0, other)))
        kept[u] = jnp.dot(tile[pl.ds(0, 4 * rows), :], w, preferred_element_type=jnp.float32)

    def chip_sum(u, step, low, size):
        at_rows = pl.ds(step * rows + low, size)
        return kept[u, at_rows, :] + pair_in[u, at_rows, :].astype(jnp.float32)

    def relay(u):
        pairs[u].wait_recv()
        for way in range(2):
            far_out[u, way] = chip_sum(u, 2, way * half, half).astype(jnp.bfloat16)
            fars[u, way] = go(
                remote(far_out.at[u, way], far_in.at[u, way], far_send.at[u, way], far_recv.at[u, way], at((1, 3)[way], core))
            )

    def neighbour(u):
        for way in range(2):
            step = (1, 3)[way]
            fars[u, way].wait_recv()
            mine, through = pl.ds((1 - way) * half, half), pl.ds(way * half, half)
            near_out[u, way, mine, :] = chip_sum(u, step, (1 - way) * half, half).astype(jnp.bfloat16)
            near_out[u, way, through, :] = (
                chip_sum(u, step, way * half, half) + far_in[u, way].astype(jnp.float32)
            ).astype(jnp.bfloat16)
            nears[u, way] = go(
                remote(near_out.at[u, way], near_in.at[u, way], near_send.at[u, way], near_recv.at[u, way], at(step, core))
            )

    def finish(u):
        result = chip_sum(u, 0, 0, rows)
        for way in range(2):
            nears[u, way].wait_recv()
            result = result + near_in[u, way].astype(jnp.float32)
        key, value = result[:, :width] * scale[...], result[:, width:] * scale[...]
        turned = key * cosine[...] + pltpu.roll(key, HEAD // 2, 1) * sine[...]
        columns = pl.ds(pl.multiple_of(((col + 8 - UNITS[u]) % 8) * width, width), width)
        key_out[:, columns] = turned.astype(jnp.bfloat16)
        value_out[:, columns] = value.astype(jnp.bfloat16)

    count = len(UNITS)
    for step in range(count + 5):
        if step == 1:
            arrive(6)
        for j in {1: (0, 1), 3: (2, 3), 5: (4, 5), 7: (6,)}.get(step, ()):
            cross(j)
        if step < count:
            multiply(step)
        for stage, lag in ((relay, 1), (neighbour, 3), (finish, 5)):
            if 0 <= step - lag < count:
                stage(step - lag)
    for copy in sent:
        copy.wait_send()


def body(tokens, norm_gain, w_key, w_value):
    rows, model = tokens.shape
    depth, width = w_key.shape
    pair = 2 * width
    half_lane = np.arange(HEAD) % (HEAD // 2)
    frequency = jnp.asarray(rope_base ** (-2.0 * half_lane / HEAD), jnp.float32).reshape(1, HEAD)
    units = len(UNITS)
    bf16, f32 = jnp.bfloat16, jnp.float32
    dma = pltpu.SemaphoreType.DMA
    anywhere = pl.BlockSpec(memory_space=pl.ANY)
    vmem = pl.BlockSpec(memory_space=pltpu.VMEM)
    out = pltpu.VMEM((rows, units * width), bf16)
    return pl.pallas_call(
        kernel,
        name="key_value",
        out_shape=(out, out),
        in_specs=[anywhere] * 5,
        out_specs=(vmem, vmem),
        scratch_shapes=[
            pltpu.VMEM((rows, model), bf16),
            pltpu.VMEM((8 * rows, depth), bf16),
            pltpu.VMEM((units, depth, pair), bf16),
            pltpu.VMEM((2, rows, depth), bf16),
            pltpu.VMEM((units, 4 * rows, pair), f32),
            pltpu.VMEM((units, 4 * rows, pair), bf16),
            pltpu.VMEM((units, 4 * rows, pair), bf16),
            pltpu.VMEM((units, 2, rows // 2, pair), bf16),
            pltpu.VMEM((units, 2, rows // 2, pair), bf16),
            pltpu.VMEM((units, 2, rows, pair), bf16),
            pltpu.VMEM((units, 2, rows, pair), bf16),
            pltpu.VMEM((rows, width), f32),
            pltpu.VMEM((rows, width), f32),
            pltpu.VMEM((rows, width), f32),
            pltpu.VMEM((1, depth), f32),
            pltpu.VMEM((1, width), f32),
            dma((6,)),
            dma((2, 7)), dma((2, 7)),
            dma((2, 7)), dma((2, 7)),
            dma((2,)), dma((2,)),
            dma((2, 4)), dma((2, 4)),
            dma((units,)), dma((units,)),
            dma((units, 2)), dma((units, 2)),
            dma((units, 2)), dma((units, 2)),
        ],
        compiler_params=pltpu.CompilerParams(collective_id=0, has_side_effects=True),
    )(tokens, norm_gain.reshape(1, model), w_key, w_value, frequency)


def solution(mesh):
    placed = (P(("dp", "row", "col"), None), P(), P("row", "col"), P("row", "col"))
    return jax.shard_map(
        body,
        mesh=mesh,
        in_specs=placed,
        out_specs=(P(("dp", "row", "col"), None), P(("dp", "row", "col"), None)),
        check_vma=False,
    )
```

```python
import jax
import jax.numpy as jnp
import numpy as np
from jax import lax
from jax.experimental import pallas as pl
from jax.experimental.pallas import tpu as pltpu
from jax.sharding import PartitionSpec as P

HEAD = 128
EPS = 1e-05
MESH = pl.DeviceIdType.MESH

rope_base = 500000.0

UNITS = (0, 1, 7, 2, 6, 3, 5, 4)
EARLY = 3


def rotation_tables(first, frequency, shape):
    lane = lax.broadcasted_iota(jnp.int32, shape, 1)
    position = first + lax.broadcasted_iota(jnp.int32, shape, 0)
    angles = position.astype(jnp.float32) * frequency
    sine = jnp.sin(angles)
    return jnp.cos(angles), jnp.where(lane < HEAD // 2, -sine, sine)


def kernel(
    tokens, gain, w_key, w_value, frequency, key_out, value_out,
    tok, tile, weights, hop, kept, pair_out, pair_in, far_out, far_in, near_out, near_in, scale, cosine, sine, own_gain, own_frequency,
    local_sem, z_send, z_recv, x_send, x_recv, hop_send, hop_recv, tile_send, tile_recv,
    pair_send, pair_recv, far_send, far_recv, near_send, near_recv,
):
    rows = tokens.shape[0]
    depth, width = w_key.shape
    half = rows // 2
    dp, row, col = lax.axis_index("dp"), lax.axis_index("row"), lax.axis_index("col")
    y, core = row // 2, row % 2
    other = 1 - core

    def at(step, which):
        return (dp, ((y + step + 4) % 4) * 2 + which, col)

    wrap_up, wrap_down = col // 7, (7 - col) // 7
    z_next = ((dp + 4 * wrap_up) % 8, row, (col + 1) % 8)
    z_prev = ((dp + 4 * wrap_down) % 8, row, (col + 7) % 8)

    x, kind_here = dp % 4, dp % 2
    x_next = (dp - x + (x + 1) % 4, row, col)
    x_prev = (dp - x + (x + 3) % 4, row, col)

    partners = [at(1, core), at(3, core), at(1, other), at(3, other), at(0, other), z_next, z_prev, x_next, x_prev]
    def features(step, which):
        index = ((y + step) % 4) * 2 + which
        return tokens.at[:, pl.ds(pl.multiple_of(index * depth, depth), depth)]

    def tile_rows(kind, step):
        return tile.at[pl.ds((kind * 4 + step) * rows, rows), :]

    own_key = pltpu.make_async_copy(w_key, weights.at[0, :, pl.ds(0, width)], local_sem.at[1])
    own_value = pltpu.make_async_copy(w_value, weights.at[0, :, pl.ds(width, width)], local_sem.at[2])
    own_tile = pltpu.make_async_copy(features(0, core), tile_rows(0, 0), local_sem.at[0])
    own_tokens = pltpu.make_async_copy(tokens, tok, local_sem.at[3])
    gains = pltpu.make_async_copy(
        gain.at[:, pl.ds(pl.multiple_of(row * depth, depth), depth)], own_gain, local_sem.at[4]
    )
    frequencies = pltpu.make_async_copy(frequency, own_frequency, local_sem.at[5])
    for copy in (own_key, own_value, own_tile, own_tokens, gains, frequencies):
        copy.start()

    barrier = pltpu.get_barrier_semaphore()
    for partner in partners:
        pl.semaphore_signal(barrier, inc=1, device_id=partner, device_id_type=MESH)
    pl.semaphore_wait(barrier, len(partners))

    sent = []

    def remote(src, dst, send, recv, device):
        return pltpu.make_async_remote_copy(
            src_ref=src, dst_ref=dst, send_sem=send, recv_sem=recv, device_id=device, device_id_type=MESH
        )

    def go(copy):
        copy.start()
        sent.append(copy)
        return copy

    def columns_of(kind):
        return pl.ds(pl.multiple_of(kind * width, width), width)

    def part(slot, j, way, kind):
        return weights.at[slot, pl.ds(((j + way) % 2) * (depth // 2), depth // 2), columns_of(kind)]

    def slot_of(way, distance):
        return distance if way == 0 else (8 - distance) % 8

    def piece(way, j):
        distance = j // 2 + 1
        return remote(
            part(slot_of(way, distance - 1), j, way, kind_here), part(slot_of(way, distance), j, way, kind_here),
            z_send.at[way, j], z_recv.at[way, j], (z_next, z_prev)[way],
        )

    def across(way, j, kind):
        block = part(slot_of(way, j // 2 + 1), j, way, kind)
        return remote(block, block, x_send.at[way, j], x_recv.at[way, j], (x_next, x_prev)[(j + way) % 2])

    own_key.wait()
    own_value.wait()
    pieces = [[piece(way, j) for j in range(7)] for way in range(2)]
    for j in range(2):
        for way in range(2):
            go(pieces[way][j])
    hops = [
        go(remote(features(2, core), hop.at[0], hop_send.at[0], hop_recv.at[0], at(1, core))),
        go(remote(features(2, other), hop.at[1], hop_send.at[1], hop_recv.at[1], at(3, core))),
    ]
    blocks = {}

    def block(kind, step):
        which = other if kind else core
        slot = (4 - step) % 4
        blocks[kind, slot] = go(
            remote(features(step, which), tile_rows(kind, slot), tile_send.at[kind, slot], tile_recv.at[kind, slot], at(step, which))
        )

    for step in (1, 3):
        block(0, step)
    block(1, 0)


    own_tokens.wait()

    def squares(i, total):
        part = tok[:, pl.ds(pl.multiple_of(i * 128, 128), 128)].astype(jnp.float32)
        return total + part * part

    total = lax.fori_loop(0, tokens.shape[1] // 128, squares, jnp.zeros((rows, 128), jnp.float32))
    mean = jnp.sum(total, axis=1, keepdims=True) / tokens.shape[1]
    scale[...] = jnp.broadcast_to(lax.rsqrt(mean + EPS), scale.shape)

    def weigh(kind, step):
        ref = tile_rows(kind, step)
        ref[...] = (ref[...].astype(jnp.float32) * own_gain[...]).astype(jnp.bfloat16)

    def arrive(j):
        for way in range(2):
            pieces[way][j].wait_recv()
            if j + 2 < 7:
                go(pieces[way][j + 2])
            go(across(way, j, kind_here))

    def cross(j):
        for way in range(2):
            across(way, j, 1 - kind_here).wait_recv()

    arrive(0)
    hops[0].wait_recv()
    blocks[0, 2] = go(remote(hop.at[0], tile_rows(0, 2), tile_send.at[0, 2], tile_recv.at[0, 2], at(1, core)))
    hops[1].wait_recv()
    blocks[1, 2] = go(remote(hop.at[1], tile_rows(1, 2), tile_send.at[1, 2], tile_recv.at[1, 2], at(3, other)))
    for step in (1, 3):
        block(1, step)
    arrive(1)
    gains.wait()
    own_tile.wait()
    weigh(0, 0)
    blocks[1, 0].wait_recv()
    weigh(1, 0)
    arrive(2)
    for slot in (1, 3):
        blocks[0, slot].wait_recv()
        weigh(0, slot)
    arrive(3)
    arrive(4)
    for kind in (0, 1):
        blocks[kind, 2].wait_recv()
        weigh(kind, 2)

    pairs, fars, nears = {}, {}, {}

    def keep(u):
        kept[u] = jnp.dot(tile[pl.ds(0, 4 * rows), :], weights[UNITS[u]], preferred_element_type=jnp.float32)

    def multiply(u):
        w = weights[UNITS[u]]
        pair_out[u] = jnp.dot(
            tile[pl.ds(4 * rows, 4 * rows), :], w, preferred_element_type=jnp.float32
        ).astype(jnp.bfloat16)
        pairs[u] = go(remote(pair_out.at[u], pair_in.at[u], pair_send.at[u], pair_recv.at[u], at(0, other)))
        if u >= EARLY:
            keep(u)

    def chip_sum(u, step, low, size):
        at_rows = pl.ds(step * rows + low, size)
        return kept[u, at_rows, :] + pair_in[u, at_rows, :].astype(jnp.float32)

    def relay(u):
        pairs[u].wait_recv()
        for way in range(2):
            far_out[u, way] = chip_sum(u, 2, way * half, half).astype(jnp.bfloat16)
            fars[u, way] = go(
                remote(far_out.at[u, way], far_in.at[u, way], far_send.at[u, way], far_recv.at[u, way], at((1, 3)[way], core))
            )

    def neighbour(u):
        for way in range(2):
            step = (1, 3)[way]
            fars[u, way].wait_recv()
            mine, through = pl.ds((1 - way) * half, half), pl.ds(way * half, half)
            near_out[u, way, mine, :] = chip_sum(u, step, (1 - way) * half, half).astype(jnp.bfloat16)
            near_out[u, way, through, :] = (
                chip_sum(u, step, way * half, half) + far_in[u, way].astype(jnp.float32)
            ).astype(jnp.bfloat16)
            nears[u, way] = go(
                remote(near_out.at[u, way], near_in.at[u, way], near_send.at[u, way], near_recv.at[u, way], at(step, core))
            )

    def finish(u):
        result = chip_sum(u, 0, 0, rows)
        for way in range(2):
            nears[u, way].wait_recv()
            result = result + near_in[u, way].astype(jnp.float32)
        key, value = result[:, :width] * scale[...], result[:, width:] * scale[...]
        turned = key * cosine[...] + pltpu.roll(key, HEAD // 2, 1) * sine[...]
        columns = pl.ds(pl.multiple_of(((col + 8 - UNITS[u]) % 8) * width, width), width)
        key_out[:, columns] = turned.astype(jnp.bfloat16)
        value_out[:, columns] = value.astype(jnp.bfloat16)

    keep(0)
    for j in (0, 1):
        cross(j)
    for u in range(1, EARLY):
        keep(u)
    for slot in (1, 3):
        blocks[1, slot].wait_recv()
        weigh(1, slot)

    count = len(UNITS)
    for step in range(count + 5):
        for j in {1: (5,), 2: (6,)}.get(step, ()):
            arrive(j)
        for j in {3: (2, 3), 5: (4, 5), 7: (6,)}.get(step, ()):
            cross(j)
        if step < count:
            multiply(step)
        if step == 3:
            frequencies.wait()
            first = (row * 8 + col) * rows
            cosine[...], sine[...] = rotation_tables(first, own_frequency[...], cosine.shape)
        for stage, lag in ((relay, 1), (neighbour, 3), (finish, 5)):
            if 0 <= step - lag < count:
                stage(step - lag)
    for copy in sent:
        copy.wait_send()


def body(tokens, norm_gain, w_key, w_value):
    rows, model = tokens.shape
    depth, width = w_key.shape
    pair = 2 * width
    half_lane = np.arange(HEAD) % (HEAD // 2)
    frequency = jnp.asarray(rope_base ** (-2.0 * half_lane / HEAD), jnp.float32).reshape(1, HEAD)
    units = len(UNITS)
    bf16, f32 = jnp.bfloat16, jnp.float32
    dma = pltpu.SemaphoreType.DMA
    anywhere = pl.BlockSpec(memory_space=pl.ANY)
    vmem = pl.BlockSpec(memory_space=pltpu.VMEM)
    out = pltpu.VMEM((rows, units * width), bf16)
    return pl.pallas_call(
        kernel,
        name="key_value",
        out_shape=(out, out),
        in_specs=[anywhere] * 5,
        out_specs=(vmem, vmem),
        scratch_shapes=[
            pltpu.VMEM((rows, model), bf16),
            pltpu.VMEM((8 * rows, depth), bf16),
            pltpu.VMEM((units, depth, pair), bf16),
            pltpu.VMEM((2, rows, depth), bf16),
            pltpu.VMEM((units, 4 * rows, pair), f32),
            pltpu.VMEM((units, 4 * rows, pair), bf16),
            pltpu.VMEM((units, 4 * rows, pair), bf16),
            pltpu.VMEM((units, 2, rows // 2, pair), bf16),
            pltpu.VMEM((units, 2, rows // 2, pair), bf16),
            pltpu.VMEM((units, 2, rows, pair), bf16),
            pltpu.VMEM((units, 2, rows, pair), bf16),
            pltpu.VMEM((rows, width), f32),
            pltpu.VMEM((rows, width), f32),
            pltpu.VMEM((rows, width), f32),
            pltpu.VMEM((1, depth), f32),
            pltpu.VMEM((1, width), f32),
            dma((6,)),
            dma((2, 7)), dma((2, 7)),
            dma((2, 7)), dma((2, 7)),
            dma((2,)), dma((2,)),
            dma((2, 4)), dma((2, 4)),
            dma((units,)), dma((units,)),
            dma((units, 2)), dma((units, 2)),
            dma((units, 2)), dma((units, 2)),
        ],
        compiler_params=pltpu.CompilerParams(collective_id=0, has_side_effects=True),
    )(tokens, norm_gain.reshape(1, model), w_key, w_value, frequency)


def solution(mesh):
    placed = (P(("dp", "row", "col"), None), P(), P("row", "col"), P("row", "col"))
    return jax.shard_map(
        body,
        mesh=mesh,
        in_specs=placed,
        out_specs=(P(("dp", "row", "col"), None), P(("dp", "row", "col"), None)),
        check_vma=False,
    )
```

```python
import jax
import jax.numpy as jnp
import numpy as np
from jax import lax
from jax.experimental import pallas as pl
from jax.experimental.pallas import tpu as pltpu
from jax.sharding import PartitionSpec as P

HEAD = 128
EPS = 1e-05
MESH = pl.DeviceIdType.MESH

rope_base = 500000.0

UNITS = (0, 1, 7, 2, 6, 3, 5, 4)
EARLY = 3


def rotation_tables(first, frequency, shape):
    lane = lax.broadcasted_iota(jnp.int32, shape, 1)
    position = first + lax.broadcasted_iota(jnp.int32, shape, 0)
    angles = position.astype(jnp.float32) * frequency
    sine = jnp.sin(angles)
    return jnp.cos(angles), jnp.where(lane < HEAD // 2, -sine, sine)


def kernel(
    tokens, gain, w_key, w_value, frequency, key_out, value_out,
    tok, tile, weights, hop, kept, pair_out, pair_in, far_out, far_in, near_out, near_in, scale, cosine, sine, own_gain, own_frequency,
    local_sem, z_send, z_recv, x_send, x_recv, hop_send, hop_recv, tile_send, tile_recv,
    pair_send, pair_recv, far_send, far_recv, near_send, near_recv,
):
    rows = tokens.shape[0]
    depth, width = w_key.shape
    half = rows // 2
    dp, row, col = lax.axis_index("dp"), lax.axis_index("row"), lax.axis_index("col")
    y, core = row // 2, row % 2
    other = 1 - core

    def at(step, which):
        return (dp, ((y + step + 4) % 4) * 2 + which, col)

    wrap_up, wrap_down = col // 7, (7 - col) // 7
    z_next = ((dp + 4 * wrap_up) % 8, row, (col + 1) % 8)
    z_prev = ((dp + 4 * wrap_down) % 8, row, (col + 7) % 8)

    x, kind_here = dp % 4, dp % 2
    x_next = (dp - x + (x + 1) % 4, row, col)
    x_prev = (dp - x + (x + 3) % 4, row, col)

    partners = [at(1, core), at(3, core), at(1, other), at(3, other), at(0, other), z_next, z_prev, x_next, x_prev]
    def features(step, which):
        index = ((y + step) % 4) * 2 + which
        return tokens.at[:, pl.ds(pl.multiple_of(index * depth, depth), depth)]

    def tile_rows(kind, step):
        return tile.at[pl.ds((kind * 4 + step) * rows, rows), :]

    own_key = pltpu.make_async_copy(w_key, weights.at[0, :, pl.ds(0, width)], local_sem.at[1])
    own_value = pltpu.make_async_copy(w_value, weights.at[0, :, pl.ds(width, width)], local_sem.at[2])
    own_tile = pltpu.make_async_copy(features(0, core), tile_rows(0, 0), local_sem.at[0])
    own_tokens = pltpu.make_async_copy(tokens, tok, local_sem.at[3])
    gains = pltpu.make_async_copy(
        gain.at[:, pl.ds(pl.multiple_of(row * depth, depth), depth)], own_gain, local_sem.at[4]
    )
    frequencies = pltpu.make_async_copy(frequency, own_frequency, local_sem.at[5])
    for copy in (own_key, own_value, own_tile, own_tokens, gains, frequencies):
        copy.start()

    barrier = pltpu.get_barrier_semaphore()
    for partner in partners:
        pl.semaphore_signal(barrier, inc=1, device_id=partner, device_id_type=MESH)
    pl.semaphore_wait(barrier, len(partners))

    sent = []

    def remote(src, dst, send, recv, device):
        return pltpu.make_async_remote_copy(
            src_ref=src, dst_ref=dst, send_sem=send, recv_sem=recv, device_id=device, device_id_type=MESH
        )

    def go(copy):
        copy.start()
        sent.append(copy)
        return copy

    def columns_of(kind):
        return pl.ds(pl.multiple_of(kind * width, width), width)

    def part(slot, j, way, kind):
        return weights.at[slot, pl.ds(((j + way) % 2) * (depth // 2), depth // 2), columns_of(kind)]

    def slot_of(way, distance):
        return distance if way == 0 else (8 - distance) % 8

    def piece(way, j):
        distance = j // 2 + 1
        return remote(
            part(slot_of(way, distance - 1), j, way, kind_here), part(slot_of(way, distance), j, way, kind_here),
            z_send.at[way, j], z_recv.at[way, j], (z_next, z_prev)[way],
        )

    def across(way, j, kind):
        block = part(slot_of(way, j // 2 + 1), j, way, kind)
        return remote(block, block, x_send.at[way, j], x_recv.at[way, j], (x_next, x_prev)[(j + way) % 2])

    own_key.wait()
    own_value.wait()
    pieces = [[piece(way, j) for j in range(7)] for way in range(2)]
    for j in range(2):
        for way in range(2):
            go(pieces[way][j])
    hops = [
        go(remote(features(2, core), hop.at[0], hop_send.at[0], hop_recv.at[0], at(1, core))),
        go(remote(features(2, other), hop.at[1], hop_send.at[1], hop_recv.at[1], at(3, core))),
    ]
    blocks = {}

    def block(kind, step):
        which = other if kind else core
        slot = (4 - step) % 4
        blocks[kind, slot] = go(
            remote(features(step, which), tile_rows(kind, slot), tile_send.at[kind, slot], tile_recv.at[kind, slot], at(step, which))
        )

    for step in (1, 3):
        block(0, step)
    block(1, 0)


    def weigh(kind, step):
        ref = tile_rows(kind, step)
        ref[...] = (ref[...].astype(jnp.float32) * own_gain[...]).astype(jnp.bfloat16)

    def arrive(j):
        for way in range(2):
            pieces[way][j].wait_recv()
            if j + 2 < 7:
                go(pieces[way][j + 2])
            go(across(way, j, kind_here))

    def cross(j):
        for way in range(2):
            across(way, j, 1 - kind_here).wait_recv()

    arrive(0)
    hops[0].wait_recv()
    blocks[0, 2] = go(remote(hop.at[0], tile_rows(0, 2), tile_send.at[0, 2], tile_recv.at[0, 2], at(1, core)))
    hops[1].wait_recv()
    blocks[1, 2] = go(remote(hop.at[1], tile_rows(1, 2), tile_send.at[1, 2], tile_recv.at[1, 2], at(3, other)))
    for step in (1, 3):
        block(1, step)
    arrive(1)
    gains.wait()
    own_tile.wait()
    weigh(0, 0)
    blocks[1, 0].wait_recv()
    weigh(1, 0)
    arrive(2)
    for slot in (1, 3):
        blocks[0, slot].wait_recv()
        weigh(0, slot)
    arrive(3)
    arrive(4)
    for kind in (0, 1):
        blocks[kind, 2].wait_recv()
        weigh(kind, 2)

    pairs, fars, nears = {}, {}, {}

    def keep(u):
        kept[u] = jnp.dot(tile[pl.ds(0, 4 * rows), :], weights[UNITS[u]], preferred_element_type=jnp.float32)

    def multiply(u):
        w = weights[UNITS[u]]
        pair_out[u] = jnp.dot(
            tile[pl.ds(4 * rows, 4 * rows), :], w, preferred_element_type=jnp.float32
        ).astype(jnp.bfloat16)
        pairs[u] = go(remote(pair_out.at[u], pair_in.at[u], pair_send.at[u], pair_recv.at[u], at(0, other)))
        if u >= EARLY:
            keep(u)

    def chip_sum(u, step, low, size):
        at_rows = pl.ds(step * rows + low, size)
        return kept[u, at_rows, :] + pair_in[u, at_rows, :].astype(jnp.float32)

    def relay(u):
        pairs[u].wait_recv()
        for way in range(2):
            far_out[u, way] = chip_sum(u, 2, way * half, half).astype(jnp.bfloat16)
            fars[u, way] = go(
                remote(far_out.at[u, way], far_in.at[u, way], far_send.at[u, way], far_recv.at[u, way], at((1, 3)[way], core))
            )

    def neighbour(u):
        for way in range(2):
            step = (1, 3)[way]
            fars[u, way].wait_recv()
            mine, through = pl.ds((1 - way) * half, half), pl.ds(way * half, half)
            near_out[u, way, mine, :] = chip_sum(u, step, (1 - way) * half, half).astype(jnp.bfloat16)
            near_out[u, way, through, :] = (
                chip_sum(u, step, way * half, half) + far_in[u, way].astype(jnp.float32)
            ).astype(jnp.bfloat16)
            nears[u, way] = go(
                remote(near_out.at[u, way], near_in.at[u, way], near_send.at[u, way], near_recv.at[u, way], at(step, core))
            )

    def finish(u):
        result = chip_sum(u, 0, 0, rows)
        for way in range(2):
            nears[u, way].wait_recv()
            result = result + near_in[u, way].astype(jnp.float32)
        key, value = result[:, :width] * scale[...], result[:, width:] * scale[...]
        turned = key * cosine[...] + pltpu.roll(key, HEAD // 2, 1) * sine[...]
        columns = pl.ds(pl.multiple_of(((col + 8 - UNITS[u]) % 8) * width, width), width)
        key_out[:, columns] = turned.astype(jnp.bfloat16)
        value_out[:, columns] = value.astype(jnp.bfloat16)

    keep(0)
    for j in (0, 1):
        cross(j)
    for u in range(1, EARLY):
        keep(u)
    for slot in (1, 3):
        blocks[1, slot].wait_recv()
        weigh(1, slot)

    def prepare_scale():
        own_tokens.wait()

        def squares(i, total):
            part = tok[:, pl.ds(pl.multiple_of(i * 128, 128), 128)].astype(jnp.float32)
            return total + part * part

        total = lax.fori_loop(0, tokens.shape[1] // 128, squares, jnp.zeros((rows, 128), jnp.float32))
        mean = jnp.sum(total, axis=1, keepdims=True) / tokens.shape[1]
        scale[...] = jnp.broadcast_to(lax.rsqrt(mean + EPS), scale.shape)

    count = len(UNITS)
    for step in range(count + 5):
        for j in {1: (5,), 2: (6,)}.get(step, ()):
            arrive(j)
        for j in {3: (2, 3), 5: (4, 5), 7: (6,)}.get(step, ()):
            cross(j)
        if step < count:
            multiply(step)
        if step == 3:
            prepare_scale()
            frequencies.wait()
            first = (row * 8 + col) * rows
            cosine[...], sine[...] = rotation_tables(first, own_frequency[...], cosine.shape)
        for stage, lag in ((relay, 1), (neighbour, 3), (finish, 5)):
            if 0 <= step - lag < count:
                stage(step - lag)
    for copy in sent:
        copy.wait_send()


def body(tokens, norm_gain, w_key, w_value):
    rows, model = tokens.shape
    depth, width = w_key.shape
    pair = 2 * width
    half_lane = np.arange(HEAD) % (HEAD // 2)
    frequency = jnp.asarray(rope_base ** (-2.0 * half_lane / HEAD), jnp.float32).reshape(1, HEAD)
    units = len(UNITS)
    bf16, f32 = jnp.bfloat16, jnp.float32
    dma = pltpu.SemaphoreType.DMA
    anywhere = pl.BlockSpec(memory_space=pl.ANY)
    vmem = pl.BlockSpec(memory_space=pltpu.VMEM)
    out = pltpu.VMEM((rows, units * width), bf16)
    return pl.pallas_call(
        kernel,
        name="key_value",
        out_shape=(out, out),
        in_specs=[anywhere] * 5,
        out_specs=(vmem, vmem),
        scratch_shapes=[
            pltpu.VMEM((rows, model), bf16),
            pltpu.VMEM((8 * rows, depth), bf16),
            pltpu.VMEM((units, depth, pair), bf16),
            pltpu.VMEM((2, rows, depth), bf16),
            pltpu.VMEM((units, 4 * rows, pair), f32),
            pltpu.VMEM((units, 4 * rows, pair), bf16),
            pltpu.VMEM((units, 4 * rows, pair), bf16),
            pltpu.VMEM((units, 2, rows // 2, pair), bf16),
            pltpu.VMEM((units, 2, rows // 2, pair), bf16),
            pltpu.VMEM((units, 2, rows, pair), bf16),
            pltpu.VMEM((units, 2, rows, pair), bf16),
            pltpu.VMEM((rows, width), f32),
            pltpu.VMEM((rows, width), f32),
            pltpu.VMEM((rows, width), f32),
            pltpu.VMEM((1, depth), f32),
            pltpu.VMEM((1, width), f32),
            dma((6,)),
            dma((2, 7)), dma((2, 7)),
            dma((2, 7)), dma((2, 7)),
            dma((2,)), dma((2,)),
            dma((2, 4)), dma((2, 4)),
            dma((units,)), dma((units,)),
            dma((units, 2)), dma((units, 2)),
            dma((units, 2)), dma((units, 2)),
        ],
        compiler_params=pltpu.CompilerParams(collective_id=0, has_side_effects=True),
    )(tokens, norm_gain.reshape(1, model), w_key, w_value, frequency)


def solution(mesh):
    placed = (P(("dp", "row", "col"), None), P(), P("row", "col"), P("row", "col"))
    return jax.shard_map(
        body,
        mesh=mesh,
        in_specs=placed,
        out_specs=(P(("dp", "row", "col"), None), P(("dp", "row", "col"), None)),
        check_vma=False,
    )
```
